256 devices in a mesh: grp: 8 (over y, x_lo), blk: 32 (over z, x_hi, core).
Axes of the slice: x: 4 (x_hi: 2, x_lo: 2; x = x_hi * 2 + x_lo), y: 4, z: 8, core: 2. Of those that a mesh axis runs over, the one named last changes fastest.
Arguments:
- student: bfloat16 [49152, 1024], P(('grp', 'blk')), parts along dimension 0, may hold values from -6 to 6
- teacher: bfloat16 [49152, 1024], P(('grp', 'blk')), parts along dimension 0, may hold values from -6 to 6
Outputs:
- grad_student: float32 [49152, 1024], P(('grp', 'blk')), parts along dimension 0
The draws below stay inside these ranges and needn't reach their ends.
There are 8 independent parts, one for each index of `grp`. The reference program is written for one: setup_inputs(seed, part) draws one part's arguments, and reference() takes and returns one part's arrays. A program takes and returns all parts, laid end to end along the dimension named above; each array names one. Nothing has to cross between parts.
All inputs are finite; a program needn't handle non-finite values.
Results may differ from the reference program's by a relative error of at most 0.01.
Values may be sent and summed in bfloat16 or wider, within the bound.
A program may use at most 128 MiB of HBM per device.

```python
import jax
import jax.numpy as jnp
from jax import lax

D = 1024
N = 6144


def shard_levels(stream_key, dims, pieces, low, largest):
    def one(dim, parts):
        draws = jax.random.uniform(jax.random.fold_in(jax.random.fold_in(stream_key, 6), dim), (parts,), jnp.float32, low / len(pieces), largest / len(pieces))
        return jnp.repeat(jnp.exp(draws), dims[dim] // parts).reshape((-1,) + (1,) * (len(dims) - dim - 1))

    loudness = one(*pieces[0])
    for cut in pieces[1:]:
        loudness = loudness * one(*cut)
    return loudness


def centred(own_key, dims, width, bound, cuts=(), dtype=jnp.bfloat16):
    entries = width * jax.random.normal(own_key, dims, jnp.float32)
    if cuts:
        entries = entries * shard_levels(own_key, dims, cuts, -0.22, 0.18)
    return jnp.clip(entries, -bound, bound).astype(dtype)


def setup_inputs(seed: int = 0, part: int = 0) -> dict:
    key_list = jax.random.split(jax.random.key(seed), 3)
    own_keys = jax.random.split(jax.random.fold_in(key_list[2], part), 3)
    return {
        "student": centred(own_keys[0], (N, D), 1.0, 6.0, ((0, 32),)),
        "teacher": centred(own_keys[1], (N, D), 1.0, 6.0, ((0, 32),)),
    }


def normalize(values):
    floats = values.astype(jnp.float32)
    norms = jnp.sqrt(lax.optimization_barrier(jnp.sum(floats * floats, axis=1, keepdims=True)) + 1e-06)
    return (floats / norms, norms)

def split_product(left, right):
    left_hi = left.astype(jnp.bfloat16)
    left_lo = (left - left_hi.astype(jnp.float32)).astype(jnp.bfloat16)
    return jnp.dot(left_hi, right, preferred_element_type=jnp.float32) + jnp.dot(left_lo, right, preferred_element_type=jnp.float32)

def reference(student, teacher):
    s_float, norm_h = normalize(student)
    s_half = s_float.astype(jnp.bfloat16)
    t_float, teacher_norm = normalize(teacher)
    t_half = t_float.astype(jnp.bfloat16)
    gram_s = jnp.dot(s_half, s_half.T, preferred_element_type=jnp.float32)
    gram_t = jnp.dot(t_half, t_half.T, preferred_element_type=jnp.float32)
    diff = gram_s - gram_t
    s_wide = s_half.astype(jnp.float32)
    product = split_product(diff, s_half)
    g_s = product * (D / jnp.sqrt(jnp.float32(N)))
    along = lax.optimization_barrier(jnp.sum(s_wide * g_s, axis=1, keepdims=True))
    return (g_s - s_wide * along) / norm_h
```

```python
import functools

import jax
import jax.numpy as jnp
from jax import lax
from jax.experimental import pallas as pl
from jax.experimental.pallas import tpu as pltpu
from jax.sharding import PartitionSpec as P

MESH = pl.DeviceIdType.MESH
D = 1024
RING = 8
HALF = RING // 2
W = D // RING
SUBS = 4
CHUNK = 4 * W + 2 * W + W // 2
SUB = CHUNK // SUBS
BF = jnp.bfloat16
F32 = jnp.float32


def kernel(
    student, teacher, out, s_own, t_own, norm, s_ext, st, tt, own, sendb, recvb, xsend, xrecv, total,
    gath, acc, core_ss, core_rs, rs_ss, rs_rs, x_ss, x_rs, ag_ss, ag_rs, fw_ss, fw_rs,
):
    rows = student.shape[0]
    blk = lax.axis_index("blk")
    z, xh, core = blk // 4, (blk // 2) % 2, blk % 2
    texts = rows * lax.axis_size("blk")
    shift = 2.0 * rows / D

    def at(dz, dx, dc):
        return {"blk": ((z + dz + RING) % RING) * 4 + ((xh + dx) % 2) * 2 + (core + dc) % 2}

    up, down, across, twin = at(1, 0, 0), at(-1, 0, 0), at(0, 1, 0), at(0, 0, 1)
    ring = {1: up, -1: down}
    barrier = pltpu.get_barrier_semaphore()
    for peer in (up, down, across, twin):
        pl.semaphore_signal(barrier, inc=1, device_id=peer, device_id_type=MESH)

    def remote(src, dst, ss, rs, peer):
        return pltpu.make_async_remote_copy(
            src_ref=src, dst_ref=dst, send_sem=ss, recv_sem=rs, device_id=peer, device_id_type=MESH
        )

    x = student[...].astype(F32)
    n = jnp.sqrt(jnp.sum(x * x, axis=1, keepdims=True) + 1e-06)
    norm[...] = jnp.broadcast_to(n, norm.shape)
    s = (x / n).astype(BF)
    s_own[...] = s
    s_ext[0, :, 0:D] = s
    s_ext[0, :, D : D + D // 2] = s[:, 0 : D // 2]
    st[0] = s.T
    y = teacher[...].astype(F32)
    m = jnp.sqrt(jnp.sum(y * y, axis=1, keepdims=True) + 1e-06)
    t = -(y / m).astype(BF)
    t_own[...] = -t
    tt[0] = t.T

    pl.semaphore_wait(barrier, 4)

    pairs = ((s_ext, 0), (st, 1), (tt, 2))
    swaps = [remote(b.at[0], b.at[1], core_ss.at[i], core_rs.at[i], twin) for b, i in pairs]
    for c in swaps:
        c.start()
    for c in swaps:
        c.wait_recv()

    eye = (
        lax.broadcasted_iota(jnp.int32, (W, W), 0) == lax.broadcasted_iota(jnp.int32, (W, W), 1)
    ).astype(F32) * jnp.where(core == 0, shift, 0.0).astype(F32)

    def mul(a, b):
        return jnp.dot(a, b, preferred_element_type=F32)

    def partial(rel):
        j = (z + rel + RING) % RING
        rj = pl.ds(pl.multiple_of(j * W, W), W)
        rh = pl.ds(pl.multiple_of(j * W + core * (W // 2), W // 2), W // 2)
        ct = pl.ds(pl.multiple_of(core * (D // 2), W), D // 2)
        cs = pl.ds(pl.multiple_of((j + 3 * core) * W, W), 2 * W)
        c2 = pl.ds(pl.multiple_of((j + 2) * W, W), W)
        mt = mul(tt[0, rj, :], s_ext[0, :, ct]) + mul(tt[1, rj, :], s_ext[1, :, ct])
        ms = mul(st[0, rj, :], s_ext[0, :, cs]) + mul(st[1, rj, :], s_ext[1, :, cs])
        m2 = mul(st[0, rh, :], s_ext[0, :, c2]) + mul(st[1, rh, :], s_ext[1, :, c2])
        parts = [mt[:, k * W : (k + 1) * W] for k in range(4)]
        parts += [ms[:, :W] - eye, ms[:, W:], m2]
        return parts

    def put(ref, parts, dtype):
        row = 0
        for p in parts:
            ref[row : row + p.shape[0], :] = p.astype(dtype)
            row += p.shape[0]

    def rows_of(u):
        return pl.ds(u * SUB, SUB)

    def lane(d):
        return 0 if d > 0 else 1

    def shares(d, u):
        return (u < SUBS // 2) == (d > 0)

    def rs(d, k, u):
        i = lane(d)
        return remote(
            sendb.at[i, k - 1, rows_of(u)], recvb.at[i, k - 1, rows_of(u)],
            rs_ss.at[i, k - 1, u], rs_rs.at[i, k - 1, u], ring[d],
        )

    far = partial(HALF)
    put(sendb.at[0, 0], far, BF)
    put(sendb.at[1, 0], far, BF)
    for u in range(SUBS):
        for d in (1, -1):
            if shares(d, u):
                rs(d, 1, u).start()
    for k in (2, 3, 4):
        for d in (1, -1):
            put(own.at[lane(d), k - 2], partial(d * (HALF + 1 - k)), F32)
    put(total, partial(0), F32)

    for k in (2, 3, 4):
        order = [(d, u) for u in range(SUBS) for d in (1, -1)]
        if k == 2:
            order = [p for p in order if not shares(*p)] + [p for p in order if shares(*p)]
        for d, u in order:
            i = lane(d)
            v = own[i, k - 2, rows_of(u), :]
            if k > 2 or shares(d, u):
                rs(d, k - 1, u).wait_recv()
                v = v + recvb[i, k - 2, rows_of(u), :].astype(F32)
            sendb[i, k - 1, rows_of(u), :] = v.astype(BF)
            rs(d, k, u).start()

    def xc(u):
        return remote(xsend.at[rows_of(u)], xrecv.at[rows_of(u)], x_ss.at[u], x_rs.at[u], across)

    for u in range(SUBS):
        v = total[rows_of(u), :]
        for d in (1, -1):
            rs(d, 4, u).wait_recv()
            v = v + recvb[lane(d), 3, rows_of(u), :].astype(F32)
        total[rows_of(u), :] = v
        xsend[rows_of(u), :] = v.astype(BF)
        xc(u).start()

    def ag(d, k, u):
        i = lane(d)
        a, b = (-d * (k - 1)) % RING, (-d * k) % RING
        return remote(
            gath.at[core, a, rows_of(u)], gath.at[core, b, rows_of(u)],
            ag_ss.at[i, k - 1, u], ag_rs.at[i, k - 1, u], ring[d],
        )

    def fw(r, u):
        ref = gath.at[core, r % RING, rows_of(u)]
        return remote(ref, ref, fw_ss.at[r % RING, u], fw_rs.at[r % RING, u], twin)

    for u in range(SUBS):
        xc(u).wait_recv()
        v = total[rows_of(u), :] + xrecv[rows_of(u), :].astype(F32)
        gath[core, 0, rows_of(u), :] = v.astype(BF)
        for d in (1, -1):
            ag(d, 1, u).start()
        fw(0, u).start()

    acc[...] = jnp.zeros_like(acc)

    def apply(r):
        r = r % RING
        for u in range(SUBS):
            fw(r, u).wait_recv()
        j = (z + r) % RING

        def block(c, k):
            return gath[c, r, k * W : (k + 1) * W, :]

        mt = jnp.concatenate([block(c, k) for c in (0, 1) for k in range(4)], axis=1)
        b2 = jnp.concatenate([gath[c, r, 6 * W : CHUNK, :] for c in (0, 1)], axis=0)
        ms = jnp.concatenate([block(0, 4), block(0, 5), b2, block(1, 4), block(1, 5)], axis=1)
        tj = t_own[:, pl.ds(pl.multiple_of(j * W, W), W)]
        sj = s_ext[0, :, pl.ds(pl.multiple_of(j * W, W), W)]
        sn = s_ext[0, :, pl.ds(pl.multiple_of((j + 1) * W, W), 3 * W)]
        acc[:, 0:D] += mul(tj, mt)
        wide = pl.ds(pl.multiple_of(j * W, W), 5 * W)
        acc[:, wide] += mul(sj, ms)
        near = pl.ds(pl.multiple_of(j * W, W), W)
        acc[:, near] += lax.dot_general(
            sn, ms[:, W : 4 * W], (((1,), (1,)), ((), ())), preferred_element_type=F32
        )

    for k in (1, 2, 3, 4):
        for u in range(SUBS):
            for d in (1, -1):
                if k < HALF or shares(d, u):
                    ag(d, k, u).wait_recv()
                    if k + 1 < HALF or (k + 1 == HALF and shares(d, u)):
                        ag(d, k + 1, u).start()
                    fw(-d * k, u).start()
        apply(k - 1)
        if k > 1:
            apply(1 - k)
    apply(HALF)

    sw = s_own[...].astype(F32)
    g = acc[:, 0:D] + sw * (shift * (texts // (2 * rows)))
    g = jnp.concatenate([g[:, : D // 2] + acc[:, D:], g[:, D // 2 :]], axis=1)
    g = g * (D / jnp.sqrt(jnp.float32(texts)))
    along = jnp.sum(sw * g, axis=1, keepdims=True)
    out[...] = (g - sw * along) / norm[:, 0:1]

    for c in swaps:
        c.wait_send()
    for u in range(SUBS):
        for d in (1, -1):
            for k in (1, 2, 3, 4):
                if k > 1 or shares(d, u):
                    rs(d, k, u).wait_send()
                if k < HALF or shares(d, u):
                    ag(d, k, u).wait_send()
        xc(u).wait_send()
        for r in range(RING):
            fw(r, u).wait_send()


def body(student, teacher):
    rows = student.shape[0]
    dma = pltpu.SemaphoreType.DMA
    return pl.pallas_call(
        kernel,
        out_shape=jax.ShapeDtypeStruct((rows, D), F32),
        in_specs=[pl.BlockSpec(memory_space=pltpu.VMEM)] * 2,
        out_specs=pl.BlockSpec(memory_space=pltpu.VMEM),
        scratch_shapes=[
            pltpu.VMEM((rows, D), BF),
            pltpu.VMEM((rows, D), BF),
            pltpu.VMEM((rows, 128), F32),
            pltpu.VMEM((2, rows, D + D // 2), BF),
            pltpu.VMEM((2, D, rows), BF),
            pltpu.VMEM((2, D, rows), BF),
            pltpu.VMEM((2, 3, CHUNK, W), F32),
            pltpu.VMEM((2, 4, CHUNK, W), BF),
            pltpu.VMEM((2, 4, CHUNK, W), BF),
            pltpu.VMEM((CHUNK, W), BF),
            pltpu.VMEM((CHUNK, W), BF),
            pltpu.VMEM((CHUNK, W), F32),
            pltpu.VMEM((2, RING, CHUNK, W), BF),
            pltpu.VMEM((rows, D + D // 2), F32),
            dma((3,)), dma((3,)),
            dma((2, 4, SUBS)), dma((2, 4, SUBS)),
            dma((SUBS,)), dma((SUBS,)),
            dma((2, 4, SUBS)), dma((2, 4, SUBS)),
            dma((RING, SUBS)), dma((RING, SUBS)),
        ],
        compiler_params=pltpu.CompilerParams(
            collective_id=0, has_side_effects=True, vmem_limit_bytes=48 * 2**20
        ),
    )(student, teacher)


def solution(mesh):
    in_specs = (P(("grp", "blk"), None), P(("grp", "blk"), None))
    out_specs = P(("grp", "blk"), None)
    return jax.shard_map(body, mesh=mesh, in_specs=in_specs, out_specs=out_specs, check_vma=False)
```
